32 devices in a mesh: group: 8 (over z, x), owner: 4 (over y, core).
Axes of the slice: x: 2, y: 2, z: 4, core: 2. Of those that a mesh axis runs over, the one named last changes fastest.
Arguments:
- embeddings: bfloat16 [32768, 1024], P(('group', 'owner')), may hold values from -2 to 2
- home_pairs: int32 [8, 4, 3, 64, 2], P('group', 'owner'), may hold values from 0 to 7, as said below
- home_count: int32 [8, 4, 3], P('group', 'owner'), may hold values from 0 to 28
- surplus_pairs: int32 [8, 4, 8, 3], P('group', 'owner'), may hold values from 0 to 7, as said below
Outputs:
- centered: bfloat16 [32768, 1024], P(('group', 'owner'))
- log_density: float32 [32768], P(('group', 'owner'))
The draws below stay inside these ranges and needn't reach their ends.
Inputs may be any that keep to these rules, and one draw needn't show every extreme that they name: `home_pairs`: for owner o of group g and distance s, the first home_count[g, o, s] slots hold distinct pairs (a, b) of block a of owner o and block b of owner (o + s) mod 4 that lie in one cluster; at distance 0 a <= b and every pair (a, a) is listed; at twice s equal to 4 only owners below 2 list pairs; later slots are ignored. `surplus_pairs`: A live entry (a, b, 1) names two blocks of the same owner in one cluster with a < b; no pair is live twice or also listed in home_pairs; dead entries are ignored.
All inputs are finite; a program needn't handle non-finite values.
Results may differ from the reference program's by a relative error of at most 0.0057.
Values may be sent and summed in bfloat16 or wider, within the bound.
A program may use at most 128 MiB of HBM per device.

```python
import jax
import jax.numpy as jnp
from jax import lax

D = 1024
BLOCK = 128
BPD = 8
SHIFTS = 3
SLOTS = 64
ROWS = 32768
N_GROUP = 8
N_OWNER = 4


topic_count = 16


def offset_ranks(group_total):
    half_way = group_total // 2
    leading = [half_way, 1, group_total - 1, half_way + 1, half_way - 1, 2]
    others = [offset for offset in range(1, group_total) if offset not in leading]
    ordered = leading + others + [0]
    table = [0] * group_total
    for place in range(group_total):
        table[ordered[place]] = place
    return jnp.array(table, dtype=jnp.int32)


def pair_plan(base_key):
    sub_keys = jax.random.split(jax.random.fold_in(base_key, 7), 2)
    heavy_owner = jax.random.randint(sub_keys[0], (N_GROUP, 1, 1), 0, N_OWNER, jnp.int32)
    light_ids = jax.random.randint(sub_keys[1], (N_GROUP, N_OWNER, BPD), 1, 1 + 6 * BPD, jnp.int32)
    owner_ids = jnp.arange(N_OWNER, dtype=jnp.int32)
    cluster = jnp.where(owner_ids[None, :, None] == heavy_owner, 0, light_ids).astype(jnp.int32)
    distance = jnp.arange(SHIFTS, dtype=jnp.int32)
    partner = (owner_ids[:, None] + distance[None, :]) % N_OWNER
    partner_cluster = cluster[:, partner]
    same_cluster = cluster[:, :, None, :, None] == partner_cluster[:, :, :, None, :]
    block_ids = jnp.arange(BPD, dtype=jnp.int32)
    upper_tri = block_ids[:, None] <= block_ids[None, :]
    strict_upper = block_ids[:, None] < block_ids[None, :]
    at_zero = (distance == 0)[None, None, :, None, None]
    at_half = (2 * distance == N_OWNER)[None, None, :, None, None]
    low_owner = (owner_ids < N_OWNER // 2)[None, :, None, None, None]
    allowed = jnp.where(at_zero, upper_tri[None, None, None], True) & (jnp.logical_not(at_half) | low_owner)
    candidate = (same_cluster & allowed).reshape(N_GROUP, N_OWNER, SHIFTS, SLOTS)
    off_pairs = (same_cluster[:, :, 0] & strict_upper).reshape(N_GROUP, N_OWNER, SLOTS)
    rank = jnp.cumsum(off_pairs.astype(jnp.int32), axis=-1) - 1
    shipped = off_pairs & (rank < N_GROUP)
    home_zero = candidate[:, :, 0] & jnp.logical_not(shipped)
    home = candidate.at[:, :, 0].set(home_zero)
    positions = jnp.arange(SLOTS, dtype=jnp.int32)
    home_key = (1 - home.astype(jnp.int32)) * SLOTS + positions
    home_order = jnp.argsort(home_key, axis=-1, stable=True).astype(jnp.int32)
    home_pairs = jnp.stack([home_order // BPD, home_order % BPD], axis=-1).astype(jnp.int32)
    home_count = jnp.sum(home.astype(jnp.int32), axis=-1, dtype=jnp.int32)
    off_key = (1 - off_pairs.astype(jnp.int32)) * SLOTS + positions
    off_order = jnp.argsort(off_key, axis=-1, stable=True).astype(jnp.int32)
    off_count = jnp.sum(off_pairs.astype(jnp.int32), axis=-1, dtype=jnp.int32)
    group_ids = jnp.arange(N_GROUP, dtype=jnp.int32)
    rank_table_small = offset_ranks(N_GROUP)
    slot_rank = rank_table_small[(group_ids[None, :] - group_ids[:, None]) % N_GROUP]
    rank_table = jnp.broadcast_to(slot_rank[:, None, :], (N_GROUP, N_OWNER, N_GROUP))
    picked = jnp.take_along_axis(off_order, rank_table, axis=-1)
    live_flag = (rank_table < off_count[..., None]).astype(jnp.int32)
    surplus = jnp.stack([picked // BPD, picked % BPD, live_flag], axis=-1).astype(jnp.int32)
    return (home_pairs, home_count, surplus)


def draw_home_pairs(key, part):
    return pair_plan(key)[0]


def draw_home_count(key, part):
    return pair_plan(key)[1]


def draw_surplus_pairs(key, part):
    return pair_plan(key)[2]


def draw_embeddings(key, part):
    sub_keys = jax.random.split(jax.random.fold_in(key, 3), 4)
    centers = jax.random.normal(sub_keys[0], (topic_count, D), jnp.float32)
    topics = jax.random.randint(sub_keys[1], (ROWS,), 0, topic_count, jnp.int32)
    noise = jax.random.normal(sub_keys[2], (ROWS, D), jnp.float32)
    spread = jax.random.uniform(sub_keys[3], (ROWS, 1), jnp.float32, 0.4, 1.6)
    vectors = centers[topics] + spread * noise
    return jnp.clip(0.25 * vectors, -2.0, 2.0).astype(jnp.bfloat16)


def setup_inputs(seed: int = 0) -> dict:
    seeds = jax.random.split(jax.random.key(seed), 5)
    return {
        "embeddings": draw_embeddings(jax.random.fold_in(seeds[4], 71), 0),
        "home_pairs": draw_home_pairs(jax.random.fold_in(seeds[4], 71), 0),
        "home_count": draw_home_count(jax.random.fold_in(seeds[4], 71), 0),
        "surplus_pairs": draw_surplus_pairs(jax.random.fold_in(seeds[4], 71), 0),
    }


sharpness = 4.0
epsilon = 1e-06
batch_pairs = 16

def unit_rows(embeddings):
    widened = embeddings.astype(jnp.float32)
    inv_rms = lax.rsqrt(lax.optimization_barrier(jnp.mean(widened * widened, axis=-1, keepdims=True)) + epsilon)
    return (widened * inv_rms).astype(jnp.bfloat16)

def round_half(value):
    return lax.optimization_barrier(value.astype(jnp.bfloat16)).astype(jnp.float32)

def pair_terms(first_block, second_block):
    first_wide = first_block.astype(jnp.float32)
    second_wide = second_block.astype(jnp.float32)
    embed_width = first_block.shape[-1]
    similarity = jnp.einsum('nid,njd->nij', first_wide, second_wide) * (1.0 / embed_width)
    kernel = jnp.exp(sharpness * (similarity - 1.0))
    kernel_low = round_half(kernel)
    to_first = jnp.einsum('nij,njd->nid', kernel_low, second_wide)
    to_second = jnp.einsum('nij,nid->njd', kernel_low, first_wide)
    return (to_first, to_second, lax.optimization_barrier(jnp.sum(kernel, axis=2)), lax.optimization_barrier(jnp.sum(kernel, axis=1)))

def add_pairs(blocks, first_ids, second_ids, live_mask, second_scale, round_terms, totals):
    pad_ids = jnp.zeros((batch_pairs,), jnp.int32)
    first_ids = jnp.concatenate([first_ids.astype(jnp.int32), pad_ids])
    second_ids = jnp.concatenate([second_ids.astype(jnp.int32), pad_ids])
    live_mask = jnp.concatenate([live_mask.astype(jnp.int32), pad_ids])
    second_scale = jnp.concatenate([second_scale.astype(jnp.float32), jnp.zeros((batch_pairs,), jnp.float32)])
    live_first = jnp.argsort(1 - live_mask, stable=True).astype(jnp.int32)
    live_count = jnp.sum(live_mask, dtype=jnp.int32)

    def step(turn_index, carry):
        near_sums, near_dens, far_sums, far_dens = carry
        picked = lax.dynamic_slice_in_dim(live_first, turn_index * batch_pairs, batch_pairs, 0)
        positions = turn_index * batch_pairs + jnp.arange(batch_pairs, dtype=jnp.int32)
        keep_mask = (positions < live_count).astype(jnp.float32)
        first_pick = first_ids[picked]
        second_pick = second_ids[picked]
        to_first, to_second, dens_first, dens_second = pair_terms(blocks[first_pick], blocks[second_pick])
        if round_terms:
            to_first = round_half(to_first)
            to_second = round_half(to_second)
            dens_first = round_half(dens_first)
            dens_second = round_half(dens_second)
        other_mask = keep_mask * second_scale[picked]
        near_sums = near_sums.at[first_pick].add(to_first * keep_mask[:, None, None])
        near_dens = near_dens.at[first_pick].add(dens_first * keep_mask[:, None])
        far_sums = far_sums.at[second_pick].add(to_second * other_mask[:, None, None])
        far_dens = far_dens.at[second_pick].add(dens_second * other_mask[:, None])
        return (near_sums, near_dens, far_sums, far_dens)
    turn_count = (live_count + batch_pairs - 1) // batch_pairs
    return lax.fori_loop(0, turn_count, step, totals)

def reference(embeddings, home_pairs, home_count, surplus_pairs):
    normed = unit_rows(embeddings)
    embed_width = normed.shape[1]
    blocks = normed.reshape(-1, BLOCK, embed_width)
    block_count = blocks.shape[0]
    near_sums = jnp.zeros((block_count, BLOCK, embed_width), jnp.float32)
    near_dens = jnp.zeros((block_count, BLOCK), jnp.float32)
    groups = jnp.arange(N_GROUP, dtype=jnp.int32)[:, None, None]
    owners = jnp.arange(N_OWNER, dtype=jnp.int32)[None, :, None]
    slot_ids = jnp.arange(SLOTS, dtype=jnp.int32)[None, None, :]
    for distance in range(N_OWNER // 2 + 1):
        pair_list = home_pairs[:, :, distance]
        partner = (owners + distance) % N_OWNER
        first_ids = ((groups * N_OWNER + owners) * BPD + pair_list[..., 0]).reshape(-1)
        second_ids = ((groups * N_OWNER + partner) * BPD + pair_list[..., 1]).reshape(-1)
        live_mask = (slot_ids < home_count[:, :, distance][..., None]).astype(jnp.int32).reshape(-1)
        if distance == 0:
            second_scale = (first_ids != second_ids).astype(jnp.float32)
        else:
            second_scale = jnp.ones(first_ids.shape, jnp.float32)
        far_sums = jnp.zeros_like(near_sums)
        far_dens = jnp.zeros_like(near_dens)
        near_sums, near_dens, far_sums, far_dens = add_pairs(blocks, first_ids, second_ids, live_mask, second_scale, False, (near_sums, near_dens, far_sums, far_dens))
        if distance == 0:
            near_sums = near_sums + far_sums
            near_dens = near_dens + far_dens
        else:
            near_sums = near_sums + round_half(far_sums)
            near_dens = near_dens + round_half(far_dens)
    first_ids = ((groups * N_OWNER + owners) * BPD + surplus_pairs[..., 0]).reshape(-1)
    second_ids = ((groups * N_OWNER + owners) * BPD + surplus_pairs[..., 1]).reshape(-1)
    live_mask = surplus_pairs[..., 2].reshape(-1)
    second_scale = jnp.ones(first_ids.shape, jnp.float32)
    far_sums = jnp.zeros_like(near_sums)
    far_dens = jnp.zeros_like(near_dens)
    near_sums, near_dens, far_sums, far_dens = add_pairs(blocks, first_ids, second_ids, live_mask, second_scale, True, (near_sums, near_dens, far_sums, far_dens))
    near_sums = near_sums + far_sums
    near_dens = near_dens + far_dens
    log_density = jnp.log(near_dens).reshape(-1)
    centered = (blocks.astype(jnp.float32) - near_sums / near_dens[..., None]).astype(jnp.bfloat16)
    return (centered.reshape(-1, embed_width), log_density)
```

```python
import functools

import jax
import jax.numpy as jnp
from jax import lax
from jax.experimental import pallas as pl
from jax.experimental.pallas import tpu as pltpu
from jax.sharding import PartitionSpec as P

BLOCK = 128
LANES = 128
FIRST = 5
EXTRA = (1, 2, 4)
RING = 8

sharpness = 4.0
epsilon = 1e-06

VMEM = pltpu.MemorySpace.VMEM
SMEM = pltpu.MemorySpace.SMEM
ANY = pl.ANY
F32 = jnp.float32
BF16 = jnp.bfloat16
I32 = jnp.int32


def kernel_of(first, second):
    width = first.shape[-1]
    similarity = lax.dot_general(first, second, (((1,), (1,)), ((), ())), preferred_element_type=F32)
    return jnp.exp(similarity * (sharpness / width) - sharpness)


def iota(shape, axis):
    return lax.broadcasted_iota(I32, shape, axis)


def flag(value):
    return jnp.where(value, 1.0, 0.0).astype(BF16)


def over_lanes(left, right):
    return lax.dot_general(
        left.astype(BF16), right.astype(BF16), (((1,), (1,)), ((), ())), preferred_element_type=F32
    )


def across(left, right):
    return jnp.dot(left.astype(BF16), right.astype(BF16), preferred_element_type=F32)


def adjacency(shifts, blocks, pairs_ref, count_ref, surplus_ref):
    slots = pairs_ref.shape[2]
    tile = jnp.zeros((blocks, LANES), F32)
    for s in range(shifts):
        live = iota((blocks, slots), 1) < count_ref[0:1, s : s + 1]
        left = flag(live & (iota((blocks, slots), 0) == pairs_ref[s, 0:1, :]))
        right = flag(iota((LANES, slots), 0) == pairs_ref[s, 1:2, :] + blocks * s)
        tile = tile + over_lanes(left, right)
    rows, lanes = iota((blocks, LANES), 0), iota((blocks, LANES), 1)
    for t in range(surplus_ref.shape[3]):
        first = surplus_ref[0, 0, :, t : t + 1]
        second = surplus_ref[0, 1, :, t : t + 1]
        live = surplus_ref[0, 2, :, t : t + 1] == 1
        tile = tile + jnp.where((rows == first) & (lanes == second) & live, 1.0, 0.0)
    return tile


def slot_plan(n, shifts, blocks, tiles_ref, every):
    lanes = iota((blocks, LANES), 1)
    rows = iota((blocks, LANES), 0)
    apart = lanes // blocks
    listed = over_lanes(
        jnp.where((apart >= 2 - rows) & (apart < shifts) & (rows < 2), 1.0, 0.0), every
    )
    need = jnp.where((lanes // blocks) % 2 == 0, listed[0:1], listed[1:2])
    named = jnp.zeros((blocks, LANES), F32)
    for q in range(n):
        column = jnp.sum(tiles_ref[q], axis=0, keepdims=True)
        column = jnp.where((apart >= 2 - q % 2) & (apart < shifts), column, 0.0)
        named = named + (pltpu.roll(column, blocks * q, 1) if q else column)
    named = named + pltpu.roll(named, LANES - blocks * n, 1)
    need = jnp.where((need + named > 0.0) & (lanes < blocks * n), 1.0, 0.0)
    left, right = iota((LANES, LANES), 0), iota((LANES, LANES), 1)
    same = left // (2 * blocks) == right // (2 * blocks)
    place = across(need, flag(same & (left < right)))
    total = across(need, flag(same))
    most = jnp.max(total, axis=1, keepdims=True)
    return need, place, most


def work_list(n, shifts, blocks, me, mine, every, place):
    chips = n // 2
    left, right = iota((LANES, LANES), 0), iota((LANES, LANES), 1)
    apart = left // blocks
    ahead = apart + me
    ahead = jnp.where(ahead >= n, ahead - n, ahead)
    move = flag((apart >= 1) & (apart < shifts) & (right == ahead * blocks + left % blocks))
    far = across(mine, move)
    turned = over_lanes(flag(left == right), every)
    lanes = iota((blocks, LANES), 1)
    owner = lanes // blocks
    behind = me - owner
    behind = jnp.where(behind < 0, behind + n, behind)
    for s in range(1, shifts):
        far = far + jnp.where((behind == s) & (owner < n), turned[s * blocks : (s + 1) * blocks], 0.0)
    step = owner // 2 - me // 2
    step = jnp.where(step < 0, step + chips, step).astype(F32)
    code = jnp.where(
        step == 0.0, (lanes % blocks).astype(F32), blocks + (step - 1.0) * (2 * blocks) + place
    )
    order = across(jnp.where(far > 0.0, 1.0, 0.0), flag(left < right))
    rest = jnp.where(far > 0.0, order, -1.0)
    work = jnp.zeros((blocks, LANES), F32)
    for j in range(blocks + (chips - 1) * 2 * blocks):
        value = jnp.sum(jnp.where(rest == float(j), code, 0.0), axis=1, keepdims=True)
        work = jnp.where(lanes == j, value, work)
    number = jnp.sum(jnp.where(far > 0.0, 1.0, 0.0), axis=1, keepdims=True)
    return jnp.where(lanes == LANES - 1, number, work).astype(I32)


def front_kernel(
    n, groups, shifts, limits, pairs_ref, count_ref, surplus_ref, emb_ref,
    chip_out, acc_out, dens_ref, pack_out, recv_ref, work_ref, level_ref,
    emb, chip, acc, pack, tiles, mask, maxima, found,
    emb_sem, push_send, push_recv, list_send, list_recv, slot_send, slot_recv,
    fwd_send, fwd_recv, max_send, max_recv, chip_sem, pack_sem, acc_sem,
):
    me = lax.axis_index("owner")
    group = lax.axis_index("group")
    blocks, _, width = emb_ref.shape
    chips = n // 2
    half = BLOCK // 2
    core = lax.rem(me, 2)
    sibling = me + 1 - 2 * core
    steps = groups.bit_length() - 1
    upper = pl.multiple_of(core * half, half)

    def partner(k):
        bit = lax.rem(group // (1 << k), 2)
        return group + (1 << k) * (1 - 2 * bit)

    barrier = pltpu.get_barrier_semaphore()
    for d in range(1, n):
        pl.semaphore_signal(barrier, inc=1, device_id={"owner": lax.rem(me + d, n)})
    for k in range(steps):
        pl.semaphore_signal(barrier, inc=1, device_id={"group": partner(k)})

    def fetch(i):
        return pltpu.make_async_copy(emb_ref.at[i], emb.at[i], emb_sem.at[i])

    def push(i):
        return pltpu.make_async_remote_copy(
            src_ref=chip.at[core * blocks + i], dst_ref=chip.at[core * blocks + i],
            send_sem=push_send.at[i], recv_sem=push_recv.at[i], device_id={"owner": sibling},
        )

    def keep(i):
        return pltpu.make_async_copy(chip.at[i], chip_out.at[i], chip_sem.at[i])

    def list_copy(d):
        return pltpu.make_async_remote_copy(
            src_ref=tiles.at[me], dst_ref=tiles.at[me],
            send_sem=list_send.at[d], recv_sem=list_recv.at[d],
            device_id={"owner": lax.rem(me + d, n)},
        )

    def slot_copy(k, j):
        return pltpu.make_async_remote_copy(
            src_ref=pack.at[j], dst_ref=recv_ref.at[chips - k - 1, j, pl.ds(upper, half)],
            send_sem=slot_send.at[k, j], recv_sem=slot_recv.at[k, j],
            device_id={"owner": lax.rem(me + 2 * k, n)},
        )

    def forward(k, j):
        return pltpu.make_async_remote_copy(
            src_ref=recv_ref.at[chips - k - 1, j, pl.ds(upper, half)],
            dst_ref=recv_ref.at[chips - k - 1, j, pl.ds(upper, half)],
            send_sem=fwd_send.at[k, j], recv_sem=fwd_recv.at[k, j], device_id={"owner": sibling},
        )

    def max_copy(k):
        return pltpu.make_async_remote_copy(
            src_ref=maxima.at[k], dst_ref=found.at[k],
            send_sem=max_send.at[k], recv_sem=max_recv.at[k], device_id={"group": partner(k)},
        )

    def save(c):
        return pltpu.make_async_copy(acc.at[pl.ds(2 * c, 2)], acc_out.at[pl.ds(2 * c, 2)], acc_sem.at[c])

    @pl.loop(0, blocks)
    def _(i):
        fetch(i).start()

    mine = adjacency(shifts, blocks, pairs_ref, count_ref, surplus_ref)
    for q in range(n, LANES // blocks):
        tiles[q] = jnp.zeros((blocks, LANES), F32)
    tiles[me] = mine

    lanes = iota((blocks, LANES), 1)
    turned = over_lanes(flag(lanes == iota((blocks, LANES), 0)), mine)
    near = jnp.where(mine[:, 0:blocks] + turned > 0.0, 1.0, 0.0)
    wide = jnp.concatenate(
        [jnp.broadcast_to(near[:, b : b + 1], (blocks, BLOCK)) for b in range(blocks)], axis=1
    )
    for a in range(blocks):
        mask[a] = wide[a : a + 1]

    def normalize(i):
        fetch(i).wait()
        values = emb[i].astype(F32)
        inv = lax.rsqrt(jnp.mean(values * values, axis=-1, keepdims=True) + epsilon)
        chip[core * blocks + i] = (values * inv).astype(BF16)

    pl.semaphore_wait(barrier, n - 1 + steps)
    for d in range(1, n):
        list_copy(d).start()

    @pl.loop(0, blocks)
    def _(i):
        normalize(i)
        push(i).start()

    for d in range(1, n):
        list_copy(d).wait_recv()
    every = tiles[...].reshape(LANES, LANES)
    need, place, most = slot_plan(n, shifts, blocks, tiles, every)
    maxima[0] = jnp.broadcast_to(most, (blocks, LANES))
    max_copy(0).start()

    here = (need > 0.0) & (lanes // (2 * blocks) == me // 2)
    rank = jnp.where(here, place, -1.0)[0:1]
    spot = (lanes % (2 * blocks)).astype(F32)[0:1]

    for i in range(blocks):
        push(i).wait_recv()

    for j in range(2 * blocks):
        index = jnp.clip(jnp.sum(jnp.where(rank == float(j), spot, 0.0)).astype(I32), 0, 2 * blocks - 1)
        pack[j] = chip[index, pl.ds(upper, half), :]
        if j < limits[0]:
            for k in range(1, chips):
                slot_copy(k, j).start()

    @pl.loop(0, 2 * blocks)
    def _(i):
        keep(i).start()

    save_pack = pltpu.make_async_copy(pack, pack_out, pack_sem)
    save_pack.start()
    work_ref[...] = work_list(n, shifts, blocks, me, mine, every, place)

    own = chip.at[pl.ds(core * blocks, blocks)]

    @pl.loop(0, blocks // 2)
    def _(c):
        full = own[...].reshape(blocks * BLOCK, width)
        rows = own[pl.ds(2 * c, 2)].reshape(2 * BLOCK, width)
        first = jnp.broadcast_to(mask[2 * c], (BLOCK, blocks * BLOCK))
        second = jnp.broadcast_to(mask[2 * c + 1], (BLOCK, blocks * BLOCK))
        weights = kernel_of(rows, full) * jnp.concatenate([first, second], axis=0)
        total = jnp.sum(weights, axis=1, keepdims=True)
        dens_ref[pl.ds(2 * c, 2)] = jnp.broadcast_to(total, (2 * BLOCK, LANES)).reshape(2, BLOCK, LANES)
        close = jnp.dot(weights.astype(BF16), full, preferred_element_type=F32)
        acc[pl.ds(2 * c, 2)] = close.astype(BF16).reshape(2, BLOCK, width)
        save(c).start()

    for k in range(steps):
        max_copy(k).wait_recv()
        maxima[k + 1] = jnp.maximum(maxima[k], found[k])
        if k + 1 < steps:
            max_copy(k + 1).start()
    most = maxima[steps]
    level = jnp.zeros_like(most)
    for limit in limits:
        level = level + jnp.where(most > float(limit), 1.0, 0.0)
    level_ref[0] = jnp.max(level).astype(I32)

    for j in range(limits[0]):
        for k in range(1, chips):
            slot_copy(k, j).wait_recv()
            forward(k, j).start()
    for i in range(blocks):
        push(i).wait_send()
    for d in range(1, n):
        list_copy(d).wait_send()
    for k in range(steps):
        max_copy(k).wait_send()
    for i in range(2 * blocks):
        keep(i).wait()
    save_pack.wait()
    for c in range(blocks // 2):
        save(c).wait()
    for j in range(limits[0]):
        for k in range(1, chips):
            slot_copy(k, j).wait_send()
            forward(k, j).wait()


def more_kernel(n, base, count, pack_ref, recv_ref, slot_send, slot_recv, fwd_send, fwd_recv):
    me = lax.axis_index("owner")
    chips = n // 2
    half = BLOCK // 2
    core = lax.rem(me, 2)
    sibling = me + 1 - 2 * core
    upper = pl.multiple_of(core * half, half)

    barrier = pltpu.get_barrier_semaphore()
    for d in range(1, n):
        pl.semaphore_signal(barrier, inc=1, device_id={"owner": lax.rem(me + d, n)})
    pl.semaphore_wait(barrier, n - 1)

    def slot_copy(k, j):
        return pltpu.make_async_remote_copy(
            src_ref=pack_ref.at[base + j], dst_ref=recv_ref.at[chips - k - 1, j, pl.ds(upper, half)],
            send_sem=slot_send.at[k, j], recv_sem=slot_recv.at[k, j],
            device_id={"owner": lax.rem(me + 2 * k, n)},
        )

    def forward(k, j):
        return pltpu.make_async_remote_copy(
            src_ref=recv_ref.at[chips - k - 1, j, pl.ds(upper, half)],
            dst_ref=recv_ref.at[chips - k - 1, j, pl.ds(upper, half)],
            send_sem=fwd_send.at[k, j], recv_sem=fwd_recv.at[k, j], device_id={"owner": sibling},
        )

    for j in range(count):
        for k in range(1, chips):
            slot_copy(k, j).start()
    for j in range(count):
        for k in range(1, chips):
            slot_copy(k, j).wait_recv()
            forward(k, j).start()
    for j in range(count):
        for k in range(1, chips):
            slot_copy(k, j).wait_send()
            forward(k, j).wait()


def finish_kernel(n, base, work_ref, chip_ref, acc_ref, dens_ref, *refs):
    recvs = refs[: 2 if base else 1]
    (out_ref, log_ref, unit, acc, dens, near, out, held, codes,
     unit_sem, acc_sem, dens_sem, held_sem, out_sem) = refs[len(recvs):]
    me = lax.axis_index("owner")
    core = lax.rem(me, 2)
    blocks = unit.shape[0]
    first = recvs[0].shape[1]

    def load(i):
        return (
            pltpu.make_async_copy(chip_ref.at[core * blocks + i], unit.at[i], unit_sem.at[i]),
            pltpu.make_async_copy(acc_ref.at[i], acc.at[i], acc_sem.at[i]),
            pltpu.make_async_copy(dens_ref.at[i], dens.at[i], dens_sem.at[i]),
        )

    def store(i):
        return pltpu.make_async_copy(out.at[i], out_ref.at[i], out_sem.at[i])

    @pl.loop(0, blocks)
    def _(i):
        for copy in load(i):
            copy.start()

    def slot(t):
        return held.at[lax.rem(t, RING)], held_sem.at[lax.rem(t, RING)]

    def fetch(t):
        code = codes[t]
        place, sem = slot(t)

        @pl.when(code < blocks)
        def _():
            pltpu.make_async_copy(chip_ref.at[(1 - core) * blocks + code], place, sem).start()

        other = jnp.maximum(code - blocks, 0)
        chip, spot = other // (2 * blocks), lax.rem(other, 2 * blocks)

        @pl.when((code >= blocks) & (spot < first))
        def _():
            pltpu.make_async_copy(recvs[0].at[chip, jnp.minimum(spot, first - 1)], place, sem).start()

        if base:
            @pl.when((code >= blocks) & (spot >= first))
            def _():
                pltpu.make_async_copy(recvs[1].at[chip, jnp.maximum(spot - first, 0)], place, sem).start()

    total = jnp.int32(0)
    starts = []
    for a in range(blocks):
        number = work_ref[a, LANES - 1]
        starts.append(total)

        @pl.loop(0, number)
        def _(t, total=total, a=a):
            codes[total + t] = work_ref[a, t]

        total = total + number
    starts.append(total)

    @pl.loop(0, jnp.minimum(total, RING))
    def _(t):
        fetch(t)

    for i in range(blocks):
        for copy in load(i):
            copy.wait()

        near[...] = acc[i].astype(F32)

        @pl.loop(starts[i], starts[i + 1])
        def _(t):
            place, sem = slot(t)
            pltpu.make_async_copy(chip_ref.at[0], place, sem).wait()
            other = place[...]
            weights = kernel_of(unit[i], other)
            dens[i] += jnp.broadcast_to(jnp.sum(weights, axis=1, keepdims=True), (BLOCK, LANES))
            near[...] += jnp.dot(weights.astype(BF16), other, preferred_element_type=F32)

            @pl.when(t + RING < total)
            def _():
                fetch(t + RING)

        density = dens[i]
        share = near[...] * (1.0 / density[:, 0:1])
        out[i] = (unit[i].astype(F32) - share).astype(BF16)
        log_ref[i] = jnp.log(density.T[0:1])
        store(i).start()

    for i in range(blocks):
        store(i).wait()


def shards(groups, embeddings, home_pairs, home_count, surplus_pairs):
    n = lax.axis_size("owner")
    chips = n // 2
    width = embeddings.shape[1]
    blocks = embeddings.shape[0] // BLOCK
    shifts, slots = home_pairs.shape[2], home_pairs.shape[3]
    most = 2 * blocks
    extra = tuple(e for e in EXTRA if FIRST + e < most) + (most - FIRST,)
    limits = (FIRST,) + tuple(FIRST + e for e in extra[:-1])

    pairs = home_pairs[0, 0].transpose(0, 2, 1)
    count = home_count[0, 0].reshape(1, shifts)
    chosen = surplus_pairs.transpose(0, 3, 1, 2)
    emb = embeddings.reshape(blocks, BLOCK, width)
    vmem = pl.BlockSpec(memory_space=VMEM)
    smem = pl.BlockSpec(memory_space=SMEM)
    anyw = pl.BlockSpec(memory_space=ANY)
    shape = jax.ShapeDtypeStruct
    dma = pltpu.SemaphoreType.DMA
    half = BLOCK // 2
    steps = groups.bit_length() - 1

    chip, acc, dens, pack, recv, work, level = pl.pallas_call(
        functools.partial(front_kernel, n, groups, shifts, limits),
        out_shape=(
            shape((2 * blocks, BLOCK, width), BF16),
            shape((blocks, BLOCK, width), BF16),
            shape((blocks, BLOCK, LANES), F32),
            shape((2 * blocks, half, width), BF16),
            shape((chips - 1, FIRST, BLOCK, width), BF16),
            shape((blocks, LANES), I32),
            shape((1,), I32),
        ),
        in_specs=[vmem, vmem, vmem, anyw],
        out_specs=(anyw, anyw, vmem, anyw, anyw, vmem, smem),
        scratch_shapes=[
            pltpu.VMEM((blocks, BLOCK, width), BF16),
            pltpu.VMEM((2 * blocks, BLOCK, width), BF16),
            pltpu.VMEM((blocks, BLOCK, width), BF16),
            pltpu.VMEM((2 * blocks, half, width), BF16),
            pltpu.VMEM((LANES // blocks, blocks, LANES), F32),
            pltpu.VMEM((blocks, 1, blocks * BLOCK), F32),
            pltpu.VMEM((steps + 1, blocks, LANES), F32),
            pltpu.VMEM((steps, blocks, LANES), F32),
            dma((blocks,)), dma((blocks,)), dma((blocks,)), dma((n,)), dma((n,)),
            dma((chips, FIRST)), dma((chips, FIRST)), dma((chips, FIRST)), dma((chips, FIRST)),
            dma((steps,)), dma((steps,)), dma((2 * blocks,)), dma, dma((blocks // 2,)),
        ],
        compiler_params=pltpu.CompilerParams(
            collective_id=0, has_side_effects=True, vmem_limit_bytes=56 * 1024 * 1024
        ),
    )(pairs, count, chosen, emb)

    def finish(base, recvs, work, chip, acc, dens):
        entries = blocks * (LANES - 1)
        return pl.pallas_call(
            functools.partial(finish_kernel, n, base),
            out_shape=(
                shape((blocks, BLOCK, width), BF16),
                shape((blocks, 1, BLOCK), F32),
            ),
            in_specs=[smem] + [anyw] * (3 + len(recvs)),
            out_specs=(anyw, vmem),
            scratch_shapes=[
                pltpu.VMEM((blocks, BLOCK, width), BF16),
                pltpu.VMEM((blocks, BLOCK, width), BF16),
                pltpu.VMEM((blocks, BLOCK, LANES), F32),
                pltpu.VMEM((BLOCK, width), F32),
                pltpu.VMEM((blocks, BLOCK, width), BF16),
                pltpu.VMEM((RING, BLOCK, width), BF16),
                pltpu.SMEM((entries,), I32),
                dma((blocks,)), dma((blocks,)), dma((blocks,)), dma((RING,)), dma((blocks,)),
            ],
            compiler_params=pltpu.CompilerParams(vmem_limit_bytes=56 * 1024 * 1024),
        )(work, chip, acc, dens, *recvs)

    def enough(work, chip, acc, dens, pack, recv):
        return finish(0, (recv,), work, chip, acc, dens)

    def with_more(rank, number, work, chip, acc, dens, pack, recv):
        later = pl.pallas_call(
            functools.partial(more_kernel, n, FIRST, number),
            out_shape=shape((chips - 1, number, BLOCK, width), BF16),
            in_specs=[anyw],
            out_specs=anyw,
            scratch_shapes=[dma((chips, number)) for _ in range(4)],
            compiler_params=pltpu.CompilerParams(collective_id=1 + rank, has_side_effects=True),
        )(pack)
        return finish(FIRST, (recv, later), work, chip, acc, dens)

    branches = [enough] + [functools.partial(with_more, rank, e) for rank, e in enumerate(extra)]
    centered, log_density = lax.switch(level[0], branches, work, chip, acc, dens, pack, recv)
    return (centered.reshape(-1, width), log_density.reshape(-1))


def solution(mesh):
    return jax.shard_map(
        functools.partial(shards, mesh.shape["group"]),
        mesh=mesh,
        in_specs=(
            P(("group", "owner"), None),
            P("group", "owner", None, None, None),
            P("group", "owner", None),
            P("group", "owner", None, None),
        ),
        out_specs=(P(("group", "owner"), None), P(("group", "owner"))),
        check_vma=False,
    )
```

```python
import functools

import jax
import jax.numpy as jnp
from jax import lax
from jax.experimental import pallas as pl
from jax.experimental.pallas import tpu as pltpu
from jax.sharding import PartitionSpec as P

BLOCK = 128
LANES = 128
FIRST = 5
EXTRA = (1, 2, 4)
EAGER = 4
VMEM_BYTES = 26 * 1024 * 1024
FRONT_BYTES = 67043328 - 39 * 256 * 1024 - 16384

sharpness = 4.0
epsilon = 1e-06

VMEM = pltpu.MemorySpace.VMEM
SMEM = pltpu.MemorySpace.SMEM
ANY = pl.ANY
F32 = jnp.float32
BF16 = jnp.bfloat16
I32 = jnp.int32


def kernel_of(first, second):
    width = first.shape[-1]
    similarity = lax.dot_general(first, second, (((1,), (1,)), ((), ())), preferred_element_type=F32)
    return jnp.exp(similarity * (sharpness / width) - sharpness)


def iota(shape, axis):
    return lax.broadcasted_iota(I32, shape, axis)


def flag(value):
    return jnp.where(value, 1.0, 0.0).astype(BF16)


def over_lanes(left, right):
    return lax.dot_general(
        left.astype(BF16), right.astype(BF16), (((1,), (1,)), ((), ())), preferred_element_type=F32
    )


def across(left, right):
    return jnp.dot(left.astype(BF16), right.astype(BF16), preferred_element_type=F32)


def adjacency(shifts, blocks, pairs_ref, count_ref, surplus_ref):
    slots = pairs_ref.shape[2]
    tile = jnp.zeros((blocks, LANES), F32)
    for s in range(shifts):
        live = iota((blocks, slots), 1) < count_ref[0:1, s : s + 1]
        left = flag(live & (iota((blocks, slots), 0) == pairs_ref[s, 0:1, :]))
        right = flag(iota((LANES, slots), 0) == pairs_ref[s, 1:2, :] + blocks * s)
        tile = tile + over_lanes(left, right)
    rows, lanes = iota((blocks, LANES), 0), iota((blocks, LANES), 1)
    for t in range(surplus_ref.shape[3]):
        first = surplus_ref[0, 0, :, t : t + 1]
        second = surplus_ref[0, 1, :, t : t + 1]
        live = surplus_ref[0, 2, :, t : t + 1] == 1
        tile = tile + jnp.where((rows == first) & (lanes == second) & live, 1.0, 0.0)
    return tile


def slot_plan(n, shifts, blocks, tiles_ref, every):
    lanes = iota((blocks, LANES), 1)
    rows = iota((blocks, LANES), 0)
    apart = lanes // blocks
    listed = over_lanes(
        jnp.where((apart >= 2 - rows) & (apart < shifts) & (rows < 2), 1.0, 0.0), every
    )
    need = jnp.where((lanes // blocks) % 2 == 0, listed[0:1], listed[1:2])
    named = jnp.zeros((blocks, LANES), F32)
    for q in range(n):
        column = jnp.sum(tiles_ref[q], axis=0, keepdims=True)
        column = jnp.where((apart >= 2 - q % 2) & (apart < shifts), column, 0.0)
        named = named + (pltpu.roll(column, blocks * q, 1) if q else column)
    named = named + pltpu.roll(named, LANES - blocks * n, 1)
    need = jnp.where((need + named > 0.0) & (lanes < blocks * n), 1.0, 0.0)
    left, right = iota((LANES, LANES), 0), iota((LANES, LANES), 1)
    same = left // (2 * blocks) == right // (2 * blocks)
    place = across(need, flag(same & (left < right)))
    total = across(need, flag(same))
    most = jnp.max(total, axis=1, keepdims=True)
    return need, place, most


def far_rows(n, shifts, blocks, me, mine, every):
    left, right = iota((LANES, LANES), 0), iota((LANES, LANES), 1)
    apart = left // blocks
    ahead = apart + me
    ahead = jnp.where(ahead >= n, ahead - n, ahead)
    move = flag((apart >= 1) & (apart < shifts) & (right == ahead * blocks + left % blocks))
    far = across(mine, move)
    turned = over_lanes(flag(left == right), every)
    lanes = iota((blocks, LANES), 1)
    owner = lanes // blocks
    behind = me - owner
    behind = jnp.where(behind < 0, behind + n, behind)
    for s in range(1, shifts):
        far = far + jnp.where((behind == s) & (owner < n), turned[s * blocks : (s + 1) * blocks], 0.0)
    return jnp.where(far > 0.0, 1.0, 0.0)


def slot_codes(n, blocks, me, place):
    chips = n // 2
    owner = iota((blocks, LANES), 1) // blocks
    step = owner // 2 - me // 2
    step = jnp.where(step < 0, step + chips, step).astype(F32)
    return jnp.where(owner < n, (step - 1.0) * (2 * blocks) + place, -1.0)


def work_list(n, blocks, far, code):
    left, right = iota((LANES, LANES), 0), iota((LANES, LANES), 1)
    late = jnp.where((far > 0.0) & (code >= 0.0), 1.0, 0.0)
    order = across(late, flag(left < right))
    rest = jnp.where(late > 0.0, order, -1.0)
    lanes = iota((blocks, LANES), 1)
    work = jnp.zeros((blocks, LANES), F32)
    for j in range((n // 2 - 1) * 2 * blocks):
        value = jnp.sum(jnp.where(rest == float(j), code, 0.0), axis=1, keepdims=True)
        work = jnp.where(lanes == j, value, work)
    number = jnp.sum(late, axis=1, keepdims=True)
    return jnp.where(lanes == LANES - 1, number, work).astype(I32)


def front_kernel(
    n, groups, shifts, limits, pairs_ref, count_ref, surplus_ref, emb_ref,
    unit, acc, dens, pack_out, recv, work_ref, level_ref,
    emb, halves, others, pack, tiles, own_mask, side_mask, maxima, found,
    emb_sem, push_send, push_recv, rest_send, rest_recv, list_send, list_recv, slot_send, slot_recv,
    fwd_send, fwd_recv, max_send, max_recv, pack_sem,
):
    me = lax.axis_index("owner")
    group = lax.axis_index("group")
    blocks, _, width = emb_ref.shape
    chips = n // 2
    half = BLOCK // 2
    core = lax.rem(me, 2)
    sibling = me + 1 - 2 * core
    steps = groups.bit_length() - 1
    first = limits[0]
    upper = pl.multiple_of(core * half, half)
    lower = pl.multiple_of((1 - core) * half, half)

    def partner(k):
        bit = lax.rem(group // (1 << k), 2)
        return group + (1 << k) * (1 - 2 * bit)

    barrier = pltpu.get_barrier_semaphore()
    for d in range(1, n):
        pl.semaphore_signal(barrier, inc=1, device_id={"owner": lax.rem(me + d, n)})
    for k in range(steps):
        pl.semaphore_signal(barrier, inc=1, device_id={"group": partner(k)})

    def fetch(i):
        return pltpu.make_async_copy(emb_ref.at[i], emb.at[i], emb_sem.at[i])

    def push(i):
        return pltpu.make_async_remote_copy(
            src_ref=unit.at[i, pl.ds(lower, half)], dst_ref=halves.at[core * blocks + i],
            send_sem=push_send.at[i], recv_sem=push_recv.at[i], device_id={"owner": sibling},
        )

    def push_rest(i):
        return pltpu.make_async_remote_copy(
            src_ref=unit.at[i, pl.ds(upper, half)], dst_ref=others.at[i],
            send_sem=rest_send.at[i], recv_sem=rest_recv.at[i], device_id={"owner": sibling},
        )

    def list_copy(d):
        return pltpu.make_async_remote_copy(
            src_ref=tiles.at[me], dst_ref=tiles.at[me],
            send_sem=list_send.at[d], recv_sem=list_recv.at[d],
            device_id={"owner": lax.rem(me + d, n)},
        )

    def slot_copy(k, j):
        return pltpu.make_async_remote_copy(
            src_ref=pack.at[j], dst_ref=recv.at[chips - k - 1, j, pl.ds(upper, half)],
            send_sem=slot_send.at[k, j], recv_sem=slot_recv.at[k, j],
            device_id={"owner": lax.rem(me + 2 * k, n)},
        )

    def forward(k, j):
        return pltpu.make_async_remote_copy(
            src_ref=recv.at[chips - k - 1, j, pl.ds(upper, half)],
            dst_ref=recv.at[chips - k - 1, j, pl.ds(upper, half)],
            send_sem=fwd_send.at[k, j], recv_sem=fwd_recv.at[k, j], device_id={"owner": sibling},
        )

    def max_copy(k):
        return pltpu.make_async_remote_copy(
            src_ref=maxima.at[k], dst_ref=found.at[k],
            send_sem=max_send.at[k], recv_sem=max_recv.at[k], device_id={"group": partner(k)},
        )

    @pl.loop(0, blocks)
    def _(i):
        fetch(i).start()

    mine = adjacency(shifts, blocks, pairs_ref, count_ref, surplus_ref)
    for q in range(n, LANES // blocks):
        tiles[q] = jnp.zeros((blocks, LANES), F32)
    tiles[me] = mine

    lanes = iota((blocks, LANES), 1)
    turned = over_lanes(flag(lanes == iota((blocks, LANES), 0)), mine)
    near = jnp.where(mine[:, 0:blocks] + turned > 0.0, 1.0, 0.0)
    wide = jnp.concatenate(
        [jnp.broadcast_to(near[:, b : b + 1], (blocks, BLOCK)) for b in range(blocks)], axis=1
    )
    for a in range(blocks):
        own_mask[a] = wide[a : a + 1]

    def normalize(i):
        fetch(i).wait()
        values = emb[i].astype(F32)
        inv = lax.rsqrt(jnp.mean(values * values, axis=-1, keepdims=True) + epsilon)
        unit[i] = (values * inv).astype(BF16)
        halves[core * blocks + i] = unit[i, pl.ds(upper, half), :]

    @pl.loop(0, EAGER)
    def _(i):
        normalize(i)

    pl.semaphore_wait(barrier, n - 1 + steps)
    for d in range(1, n):
        list_copy(d).start()

    @pl.loop(0, EAGER)
    def _(i):
        push(i).start()

    @pl.loop(EAGER, blocks)
    def _(i):
        normalize(i)
        push(i).start()

    @pl.loop(0, blocks)
    def _(i):
        push_rest(i).start()

    for d in range(1, n):
        list_copy(d).wait_recv()
    every = tiles[...].reshape(LANES, LANES)
    need, place, most = slot_plan(n, shifts, blocks, tiles, every)
    maxima[0] = jnp.broadcast_to(most, (blocks, LANES))
    max_copy(0).start()

    here = (need > 0.0) & (lanes // (2 * blocks) == me // 2)
    rank = jnp.where(here, place, -1.0)[0:1]
    spot = (lanes % (2 * blocks)).astype(F32)[0:1]

    for i in range(blocks):
        push(i).wait_recv()

    for j in range(2 * blocks):
        index = jnp.sum(jnp.where(rank == float(j), spot, 0.0)).astype(I32)
        pack[j] = halves[jnp.clip(index, 0, 2 * blocks - 1)]
        if j < first:
            for k in range(1, chips):
                slot_copy(k, j).start()

    save_pack = pltpu.make_async_copy(pack, pack_out, pack_sem)
    save_pack.start()

    far = far_rows(n, shifts, blocks, me, mine, every)
    code = slot_codes(n, blocks, me, place)
    work_ref[...] = work_list(n, blocks, far, code)
    left, right = iota((LANES, LANES), 0), iota((LANES, LANES), 1)
    side = across(far, flag((left == sibling * blocks + right) & (right < blocks)))
    two = lanes >= half
    wide = jnp.concatenate(
        [
            jnp.where(two, side[:, b + 1 : b + 2], side[:, b : b + 1])
            for b in range(0, blocks, 2)
        ],
        axis=1,
    )
    for a in range(blocks):
        side_mask[a] = wide[a : a + 1]
    def pick(mask, c):
        size = mask.shape[-1]
        return jnp.concatenate(
            [jnp.broadcast_to(mask[2 * c + e], (BLOCK, size)) for e in range(2)], axis=0
        )

    def products(rows, full, chosen):
        weights = kernel_of(rows, full) * chosen
        total = jnp.sum(weights, axis=1, keepdims=True)
        total = jnp.broadcast_to(total, (2 * BLOCK, LANES)).reshape(2, BLOCK, LANES)
        close = jnp.dot(weights.astype(BF16), full, preferred_element_type=F32)
        return total, close.reshape(2, BLOCK, width)

    @pl.loop(0, blocks // 2)
    def _(c):
        rows = unit[pl.ds(2 * c, 2)].reshape(2 * BLOCK, width)
        total, close = products(rows, unit[...].reshape(blocks * BLOCK, width), pick(own_mask, c))
        dens[pl.ds(2 * c, 2)] = total
        acc[pl.ds(2 * c, 2)] = close

    def widen(k):
        max_copy(k).wait_recv()
        maxima[k + 1] = jnp.maximum(maxima[k], found[k])
        if k + 1 < steps:
            max_copy(k + 1).start()

    def pass_on(j):
        for k in range(1, chips):
            slot_copy(k, j).wait_recv()
            forward(k, j).start()

    widen(0)
    for i in range(blocks):
        push_rest(i).wait_recv()

    @pl.loop(0, blocks // 2)
    def _(c):
        rows = unit[pl.ds(2 * c, 2)].reshape(2 * BLOCK, width)
        side = halves[pl.ds((1 - core) * blocks, blocks)].reshape(blocks * half, width)
        full = jnp.concatenate([side, others[...].reshape(blocks * half, width)], axis=0)
        beside = pick(side_mask, c)
        total, close = products(rows, full, jnp.concatenate([beside, beside], axis=1))
        dens[pl.ds(2 * c, 2)] += total
        acc[pl.ds(2 * c, 2)] += close

    for k in range(1, steps):
        widen(k)
        if k < first:
            pass_on(k - 1)
    most = maxima[steps]
    level = jnp.zeros_like(most)
    for limit in limits:
        level = level + jnp.where(most > float(limit), 1.0, 0.0)
    level_ref[0] = jnp.max(level).astype(I32)
    for j in range(min(steps, first) - 1, first):
        pass_on(j)
    for i in range(blocks):
        push(i).wait_send()
        push_rest(i).wait_send()
    for d in range(1, n):
        list_copy(d).wait_send()
    for k in range(steps):
        max_copy(k).wait_send()
    save_pack.wait()
    for j in range(first):
        for k in range(1, chips):
            slot_copy(k, j).wait_send()
            forward(k, j).wait()


def more_kernel(n, base, count, pack_ref, recv_ref, slot_send, slot_recv, fwd_send, fwd_recv):
    me = lax.axis_index("owner")
    chips = n // 2
    half = BLOCK // 2
    core = lax.rem(me, 2)
    sibling = me + 1 - 2 * core
    upper = pl.multiple_of(core * half, half)

    barrier = pltpu.get_barrier_semaphore()
    for d in range(1, n):
        pl.semaphore_signal(barrier, inc=1, device_id={"owner": lax.rem(me + d, n)})
    pl.semaphore_wait(barrier, n - 1)

    def slot_copy(k, j):
        return pltpu.make_async_remote_copy(
            src_ref=pack_ref.at[base + j], dst_ref=recv_ref.at[chips - k - 1, j, pl.ds(upper, half)],
            send_sem=slot_send.at[k, j], recv_sem=slot_recv.at[k, j],
            device_id={"owner": lax.rem(me + 2 * k, n)},
        )

    def forward(k, j):
        return pltpu.make_async_remote_copy(
            src_ref=recv_ref.at[chips - k - 1, j, pl.ds(upper, half)],
            dst_ref=recv_ref.at[chips - k - 1, j, pl.ds(upper, half)],
            send_sem=fwd_send.at[k, j], recv_sem=fwd_recv.at[k, j], device_id={"owner": sibling},
        )

    for j in range(count):
        for k in range(1, chips):
            slot_copy(k, j).start()
    for j in range(count):
        for k in range(1, chips):
            slot_copy(k, j).wait_recv()
            forward(k, j).start()
    for j in range(count):
        for k in range(1, chips):
            slot_copy(k, j).wait_send()
            forward(k, j).wait()


def finish_kernel(blocks, base, work_ref, unit, acc, dens, *refs):
    recvs = refs[: 2 if base else 1]
    out_ref, log_ref, near, reach, out, out_sem = refs[len(recvs):]
    first = recvs[0].shape[1]

    def store(i):
        return pltpu.make_async_copy(out.at[i], out_ref.at[i], out_sem.at[i])

    def meet(i, other):
        weights = kernel_of(unit[i], other)
        reach[...] += jnp.broadcast_to(jnp.sum(weights, axis=1, keepdims=True), (BLOCK, LANES))
        near[...] += jnp.dot(weights.astype(BF16), other, preferred_element_type=F32)

    def block(i, density):
        number = work_ref[i, LANES - 1]
        near[...] = acc[i]
        reach[...] = dens[i]

        @pl.loop(0, number)
        def _(t):
            code = work_ref[i, t]
            chip, spot = code // (2 * blocks), lax.rem(code, 2 * blocks)
            if base:
                @pl.when(spot < first)
                def _():
                    meet(i, recvs[0][chip, jnp.minimum(spot, first - 1)])

                @pl.when(spot >= first)
                def _():
                    meet(i, recvs[1][chip, jnp.maximum(spot - first, 0)])
            else:
                meet(i, recvs[0][chip, jnp.minimum(spot, first - 1)])

        sums = reach[...]
        share = near[...] * (1.0 / sums[:, 0:1])
        out[i] = (unit[i].astype(F32) - share).astype(BF16)
        store(i).start()
        return jnp.where(iota((BLOCK, LANES), 1) == i, sums, density)

    density = lax.fori_loop(0, blocks, block, jnp.ones((BLOCK, LANES), F32))
    log_ref[...] = jnp.log(density.T[0:blocks])

    for i in range(blocks):
        store(i).wait()


def shards(groups, embeddings, home_pairs, home_count, surplus_pairs):
    n = lax.axis_size("owner")
    chips = n // 2
    width = embeddings.shape[1]
    blocks = embeddings.shape[0] // BLOCK
    shifts = home_pairs.shape[2]
    most = 2 * blocks
    extra = tuple(e for e in EXTRA if FIRST + e < most) + (most - FIRST,)
    limits = (FIRST,) + tuple(FIRST + e for e in extra[:-1])

    pairs = home_pairs[0, 0].transpose(0, 2, 1)
    count = home_count[0, 0].reshape(1, shifts)
    chosen = surplus_pairs.transpose(0, 3, 1, 2)
    emb = embeddings.reshape(blocks, BLOCK, width)
    vmem = pl.BlockSpec(memory_space=VMEM)
    smem = pl.BlockSpec(memory_space=SMEM)
    anyw = pl.BlockSpec(memory_space=ANY)
    shape = jax.ShapeDtypeStruct
    dma = pltpu.SemaphoreType.DMA
    half = BLOCK // 2
    steps = groups.bit_length() - 1

    unit, acc, dens, pack, recv, work, level = pl.pallas_call(
        functools.partial(front_kernel, n, groups, shifts, limits),
        out_shape=(
            shape((blocks, BLOCK, width), BF16),
            shape((blocks, BLOCK, width), F32),
            shape((blocks, BLOCK, LANES), F32),
            shape((2 * blocks, half, width), BF16),
            shape((chips - 1, FIRST, BLOCK, width), BF16),
            shape((blocks, LANES), I32),
            shape((1,), I32),
        ),
        in_specs=[vmem, vmem, vmem, pl.BlockSpec(memory_space=pltpu.MemorySpace.HBM)],
        out_specs=(vmem, vmem, vmem, anyw, vmem, vmem, smem),
        scratch_shapes=[
            pltpu.VMEM((blocks, BLOCK, width), BF16),
            pltpu.VMEM((2 * blocks, half, width), BF16),
            pltpu.VMEM((blocks, half, width), BF16),
            pltpu.VMEM((2 * blocks, half, width), BF16),
            pltpu.VMEM((LANES // blocks, blocks, LANES), F32),
            pltpu.VMEM((blocks, 1, blocks * BLOCK), F32),
            pltpu.VMEM((blocks, 1, blocks * half), F32),
            pltpu.VMEM((steps + 1, blocks, LANES), F32),
            pltpu.VMEM((steps, blocks, LANES), F32),
            dma((blocks,)), dma((blocks,)), dma((blocks,)), dma((blocks,)), dma((blocks,)),
            dma((n,)), dma((n,)),
            dma((chips, FIRST)), dma((chips, FIRST)), dma((chips, FIRST)), dma((chips, FIRST)),
            dma((steps,)), dma((steps,)), dma,
        ],
        compiler_params=pltpu.CompilerParams(
            collective_id=0, has_side_effects=True, vmem_limit_bytes=FRONT_BYTES
        ),
    )(pairs, count, chosen, emb)

    def finish(base, recvs, work, unit, acc, dens):
        centered, log_density = pl.pallas_call(
            functools.partial(finish_kernel, blocks, base),
            out_shape=(
                shape((blocks, BLOCK, width), BF16),
                shape((blocks, BLOCK), F32),
            ),
            in_specs=[smem] + [vmem] * (3 + len(recvs)),
            out_specs=(anyw, vmem),
            scratch_shapes=[
                pltpu.VMEM((BLOCK, width), F32),
                pltpu.VMEM((BLOCK, LANES), F32),
                pltpu.VMEM((blocks, BLOCK, width), BF16),
                dma((blocks,)),
            ],
            compiler_params=pltpu.CompilerParams(vmem_limit_bytes=VMEM_BYTES),
        )(work, unit, acc, dens, *recvs)
        return centered.reshape(-1, width), log_density.reshape(-1)

    def enough(work, unit, acc, dens, pack, recv):
        return finish(0, (recv,), work, unit, acc, dens)

    def with_more(rank, number, work, unit, acc, dens, pack, recv):
        later = pl.pallas_call(
            functools.partial(more_kernel, n, FIRST, number),
            out_shape=shape((chips - 1, number, BLOCK, width), BF16),
            in_specs=[anyw],
            out_specs=anyw,
            scratch_shapes=[dma((chips, number)) for _ in range(4)],
            compiler_params=pltpu.CompilerParams(
                collective_id=1 + rank, has_side_effects=True, vmem_limit_bytes=4 * 1024 * 1024
            ),
        )(pack)
        return finish(FIRST, (recv, later), work, unit, acc, dens)

    branches = [enough] + [functools.partial(with_more, rank, e) for rank, e in enumerate(extra)]
    return lax.switch(level[0], branches, work, unit, acc, dens, pack, recv)


def solution(mesh):
    return jax.shard_map(
        functools.partial(shards, mesh.shape["group"]),
        mesh=mesh,
        in_specs=(
            P(("group", "owner"), None),
            P("group", "owner", None, None, None),
            P("group", "owner", None),
            P("group", "owner", None, None),
        ),
        out_specs=(P(("group", "owner"), None), P(("group", "owner"))),
        check_vma=False,
    )
```

```python
import functools

import jax
import jax.numpy as jnp
from jax import lax
from jax.experimental import pallas as pl
from jax.experimental.pallas import tpu as pltpu
from jax.sharding import PartitionSpec as P

BLOCK = 128
LANES = 128
FIRST = 5
EXTRA = (1, 2, 4)
EAGER = 4
VMEM_BYTES = 26 * 1024 * 1024
FRONT_BYTES = 67043328 - 40 * 256 * 1024

sharpness = 4.0
epsilon = 1e-06

VMEM = pltpu.MemorySpace.VMEM
SMEM = pltpu.MemorySpace.SMEM
ANY = pl.ANY
F32 = jnp.float32
BF16 = jnp.bfloat16
I32 = jnp.int32


def kernel_of(first, second):
    width = first.shape[-1]
    similarity = lax.dot_general(first, second, (((1,), (1,)), ((), ())), preferred_element_type=F32)
    return jnp.exp(similarity * (sharpness / width) - sharpness)


def iota(shape, axis):
    return lax.broadcasted_iota(I32, shape, axis)


def flag(value):
    return jnp.where(value, 1.0, 0.0).astype(BF16)


def over_lanes(left, right):
    return lax.dot_general(
        left.astype(BF16), right.astype(BF16), (((1,), (1,)), ((), ())), preferred_element_type=F32
    )


def across(left, right):
    return jnp.dot(left.astype(BF16), right.astype(BF16), preferred_element_type=F32)


def adjacency(shifts, blocks, pairs_ref, count_ref, surplus_ref):
    slots = pairs_ref.shape[2]
    tile = jnp.zeros((blocks, LANES), F32)
    for s in range(shifts):
        live = iota((blocks, slots), 1) < count_ref[0:1, s : s + 1]
        left = flag(live & (iota((blocks, slots), 0) == pairs_ref[s, 0:1, :]))
        right = flag(iota((LANES, slots), 0) == pairs_ref[s, 1:2, :] + blocks * s)
        tile = tile + over_lanes(left, right)
    rows, lanes = iota((blocks, LANES), 0), iota((blocks, LANES), 1)
    for t in range(surplus_ref.shape[3]):
        first = surplus_ref[0, 0, :, t : t + 1]
        second = surplus_ref[0, 1, :, t : t + 1]
        live = surplus_ref[0, 2, :, t : t + 1] == 1
        tile = tile + jnp.where((rows == first) & (lanes == second) & live, 1.0, 0.0)
    return tile


def slot_plan(n, shifts, blocks, tiles_ref, every):
    lanes = iota((blocks, LANES), 1)
    rows = iota((blocks, LANES), 0)
    apart = lanes // blocks
    listed = over_lanes(
        jnp.where((apart >= 2 - rows) & (apart < shifts) & (rows < 2), 1.0, 0.0), every
    )
    need = jnp.where((lanes // blocks) % 2 == 0, listed[0:1], listed[1:2])
    named = jnp.zeros((blocks, LANES), F32)
    for q in range(n):
        column = jnp.sum(tiles_ref[q], axis=0, keepdims=True)
        column = jnp.where((apart >= 2 - q % 2) & (apart < shifts), column, 0.0)
        named = named + (pltpu.roll(column, blocks * q, 1) if q else column)
    named = named + pltpu.roll(named, LANES - blocks * n, 1)
    need = jnp.where((need + named > 0.0) & (lanes < blocks * n), 1.0, 0.0)
    left, right = iota((LANES, LANES), 0), iota((LANES, LANES), 1)
    same = left // (2 * blocks) == right // (2 * blocks)
    place = across(need, flag(same & (left < right)))
    total = across(need, flag(same))
    most = jnp.max(total, axis=1, keepdims=True)
    return need, place, most


def far_rows(n, shifts, blocks, me, mine, every):
    left, right = iota((LANES, LANES), 0), iota((LANES, LANES), 1)
    apart = left // blocks
    ahead = apart + me
    ahead = jnp.where(ahead >= n, ahead - n, ahead)
    move = flag((apart >= 1) & (apart < shifts) & (right == ahead * blocks + left % blocks))
    far = across(mine, move)
    turned = over_lanes(flag(left == right), every)
    lanes = iota((blocks, LANES), 1)
    owner = lanes // blocks
    behind = me - owner
    behind = jnp.where(behind < 0, behind + n, behind)
    for s in range(1, shifts):
        far = far + jnp.where((behind == s) & (owner < n), turned[s * blocks : (s + 1) * blocks], 0.0)
    return jnp.where(far > 0.0, 1.0, 0.0)


def slot_codes(n, blocks, me, place):
    chips = n // 2
    owner = iota((blocks, LANES), 1) // blocks
    step = owner // 2 - me // 2
    step = jnp.where(step < 0, step + chips, step).astype(F32)
    return jnp.where(owner < n, (step - 1.0) * (2 * blocks) + place, -1.0)


def work_list(n, blocks, far, code):
    left, right = iota((LANES, LANES), 0), iota((LANES, LANES), 1)
    late = jnp.where((far > 0.0) & (code >= 0.0), 1.0, 0.0)
    order = across(late, flag(left < right))
    rest = jnp.where(late > 0.0, order, -1.0)
    lanes = iota((blocks, LANES), 1)
    work = jnp.zeros((blocks, LANES), F32)
    for j in range((n // 2 - 1) * 2 * blocks):
        value = jnp.sum(jnp.where(rest == float(j), code, 0.0), axis=1, keepdims=True)
        work = jnp.where(lanes == j, value, work)
    number = jnp.sum(late, axis=1, keepdims=True)
    return jnp.where(lanes == LANES - 1, number, work).astype(I32)


def front_kernel(
    n, groups, shifts, limits, pairs_ref, count_ref, surplus_ref, emb_ref,
    unit, acc, dens, pack_out, recv, work_ref, level_ref,
    emb, halves, others, pack, tiles, own_mask, side_mask, maxima, found,
    emb_sem, push_send, push_recv, rest_send, rest_recv, list_send, list_recv, slot_send, slot_recv,
    fwd_send, fwd_recv, max_send, max_recv, pack_sem,
):
    me = lax.axis_index("owner")
    group = lax.axis_index("group")
    blocks, _, width = emb_ref.shape
    chips = n // 2
    half = BLOCK // 2
    core = lax.rem(me, 2)
    sibling = me + 1 - 2 * core
    steps = groups.bit_length() - 1
    first = limits[0]
    upper = pl.multiple_of(core * half, half)
    lower = pl.multiple_of((1 - core) * half, half)

    def partner(k):
        bit = lax.rem(group // (1 << k), 2)
        return group + (1 << k) * (1 - 2 * bit)

    barrier = pltpu.get_barrier_semaphore()
    for d in range(1, n):
        pl.semaphore_signal(barrier, inc=1, device_id={"owner": lax.rem(me + d, n)})
    for k in range(steps):
        pl.semaphore_signal(barrier, inc=1, device_id={"group": partner(k)})

    def fetch(i):
        return pltpu.make_async_copy(emb_ref.at[i], emb.at[i], emb_sem.at[i])

    def push(i):
        return pltpu.make_async_remote_copy(
            src_ref=unit.at[i, pl.ds(lower, half)], dst_ref=halves.at[core * blocks + i],
            send_sem=push_send.at[i], recv_sem=push_recv.at[i], device_id={"owner": sibling},
        )

    def push_rest(i):
        return pltpu.make_async_remote_copy(
            src_ref=unit.at[i, pl.ds(upper, half)], dst_ref=others.at[i],
            send_sem=rest_send.at[i], recv_sem=rest_recv.at[i], device_id={"owner": sibling},
        )

    def list_copy(d):
        return pltpu.make_async_remote_copy(
            src_ref=tiles.at[me], dst_ref=tiles.at[me],
            send_sem=list_send.at[d], recv_sem=list_recv.at[d],
            device_id={"owner": lax.rem(me + d, n)},
        )

    def slot_copy(k, j):
        return pltpu.make_async_remote_copy(
            src_ref=pack.at[j], dst_ref=recv.at[chips - k - 1, j, pl.ds(upper, half)],
            send_sem=slot_send.at[k, j], recv_sem=slot_recv.at[k, j],
            device_id={"owner": lax.rem(me + 2 * k, n)},
        )

    def forward(k, j):
        return pltpu.make_async_remote_copy(
            src_ref=recv.at[chips - k - 1, j, pl.ds(upper, half)],
            dst_ref=recv.at[chips - k - 1, j, pl.ds(upper, half)],
            send_sem=fwd_send.at[k, j], recv_sem=fwd_recv.at[k, j], device_id={"owner": sibling},
        )

    def max_copy(k):
        return pltpu.make_async_remote_copy(
            src_ref=maxima.at[k], dst_ref=found.at[k],
            send_sem=max_send.at[k], recv_sem=max_recv.at[k], device_id={"group": partner(k)},
        )

    @pl.loop(0, blocks)
    def _(i):
        fetch(i).start()

    mine = adjacency(shifts, blocks, pairs_ref, count_ref, surplus_ref)
    for q in range(n, LANES // blocks):
        tiles[q] = jnp.zeros((blocks, LANES), F32)
    tiles[me] = mine

    lanes = iota((blocks, LANES), 1)
    turned = over_lanes(flag(lanes == iota((blocks, LANES), 0)), mine)
    near = jnp.where(mine[:, 0:blocks] + turned > 0.0, 1.0, 0.0)
    wide = jnp.concatenate(
        [jnp.broadcast_to(near[:, b : b + 1], (blocks, BLOCK)) for b in range(blocks)], axis=1
    )
    for a in range(blocks):
        own_mask[a] = wide[a : a + 1]

    def normalize(i):
        fetch(i).wait()
        values = emb[i].astype(F32)
        inv = lax.rsqrt(jnp.mean(values * values, axis=-1, keepdims=True) + epsilon)
        unit[i] = (values * inv).astype(BF16)
        halves[core * blocks + i] = unit[i, pl.ds(upper, half), :]

    @pl.loop(0, EAGER)
    def _(i):
        normalize(i)

    pl.semaphore_wait(barrier, n - 1 + steps)
    for d in range(1, n):
        list_copy(d).start()

    @pl.loop(0, EAGER)
    def _(i):
        push(i).start()

    @pl.loop(EAGER, blocks)
    def _(i):
        normalize(i)
        push(i).start()

    @pl.loop(0, blocks)
    def _(i):
        push_rest(i).start()

    for d in range(1, n):
        list_copy(d).wait_recv()
    every = tiles[...].reshape(LANES, LANES)
    need, place, most = slot_plan(n, shifts, blocks, tiles, every)
    maxima[0] = jnp.broadcast_to(most, (blocks, LANES))
    max_copy(0).start()

    here = (need > 0.0) & (lanes // (2 * blocks) == me // 2)
    rank = jnp.where(here, place, -1.0)[0:1]
    spot = (lanes % (2 * blocks)).astype(F32)[0:1]

    for i in range(blocks):
        push(i).wait_recv()

    for j in range(2 * blocks):
        index = jnp.sum(jnp.where(rank == float(j), spot, 0.0)).astype(I32)
        pack[j] = halves[jnp.clip(index, 0, 2 * blocks - 1)]
        if j < first:
            for k in range(1, chips):
                slot_copy(k, j).start()

    save_pack = pltpu.make_async_copy(pack, pack_out, pack_sem)
    save_pack.start()

    far = far_rows(n, shifts, blocks, me, mine, every)
    code = slot_codes(n, blocks, me, place)
    work_ref[...] = work_list(n, blocks, far, code)
    left, right = iota((LANES, LANES), 0), iota((LANES, LANES), 1)
    side = across(far, flag((left == sibling * blocks + right) & (right < blocks)))
    two = lanes >= half
    wide = jnp.concatenate(
        [
            jnp.where(two, side[:, b + 1 : b + 2], side[:, b : b + 1])
            for b in range(0, blocks, 2)
        ],
        axis=1,
    )
    for a in range(blocks):
        side_mask[a] = wide[a : a + 1]
    def pick(mask, c):
        size = mask.shape[-1]
        return jnp.concatenate(
            [jnp.broadcast_to(mask[2 * c + e], (BLOCK, size)) for e in range(2)], axis=0
        )

    def products(rows, full, chosen):
        weights = kernel_of(rows, full) * chosen
        total = jnp.sum(weights, axis=1, keepdims=True)
        total = jnp.broadcast_to(total, (2 * BLOCK, LANES)).reshape(2, BLOCK, LANES)
        close = jnp.dot(weights.astype(BF16), full, preferred_element_type=F32)
        return total, close.reshape(2, BLOCK, width)

    def own_products(c):
        rows = unit[pl.ds(2 * c, 2)].reshape(2 * BLOCK, width)
        total, close = products(rows, unit[...].reshape(blocks * BLOCK, width), pick(own_mask, c))
        dens[pl.ds(2 * c, 2)] = total
        acc[pl.ds(2 * c, 2)] = close

    def side_products(c):
        rows = unit[pl.ds(2 * c, 2)].reshape(2 * BLOCK, width)
        side = halves[pl.ds((1 - core) * blocks, blocks)].reshape(blocks * half, width)
        full = jnp.concatenate([side, others[...].reshape(blocks * half, width)], axis=0)
        beside = pick(side_mask, c)
        total, close = products(rows, full, jnp.concatenate([beside, beside], axis=1))
        dens[pl.ds(2 * c, 2)] += total
        acc[pl.ds(2 * c, 2)] += close

    def widen(k):
        max_copy(k).wait_recv()
        maxima[k + 1] = jnp.maximum(maxima[k], found[k])
        if k + 1 < steps:
            max_copy(k + 1).start()

    def pass_on(j):
        for k in range(1, chips):
            slot_copy(k, j).wait_recv()
            forward(k, j).start()

    parts = blocks // 2
    for turn in range(4):
        if turn == 2:
            for i in range(blocks):
                push_rest(i).wait_recv()

        middle = parts // 2
        begin, end = ((0, middle), (middle, parts))[turn % 2]

        @pl.loop(begin, end)
        def _(c, turn=turn):
            (own_products if turn < 2 else side_products)(c)

        if turn < steps:
            widen(turn)

    for k in range(4, steps):
        widen(k)
    most = maxima[steps]
    level = jnp.zeros_like(most)
    for limit in limits:
        level = level + jnp.where(most > float(limit), 1.0, 0.0)
    level_ref[0] = jnp.max(level).astype(I32)
    for j in range(first):
        pass_on(j)
    for i in range(blocks):
        push(i).wait_send()
        push_rest(i).wait_send()
    for d in range(1, n):
        list_copy(d).wait_send()
    for k in range(steps):
        max_copy(k).wait_send()
    save_pack.wait()
    for j in range(first):
        for k in range(1, chips):
            slot_copy(k, j).wait_send()
            forward(k, j).wait()


def more_kernel(n, base, count, pack_ref, recv_ref, slot_send, slot_recv, fwd_send, fwd_recv):
    me = lax.axis_index("owner")
    chips = n // 2
    half = BLOCK // 2
    core = lax.rem(me, 2)
    sibling = me + 1 - 2 * core
    upper = pl.multiple_of(core * half, half)

    barrier = pltpu.get_barrier_semaphore()
    for d in range(1, n):
        pl.semaphore_signal(barrier, inc=1, device_id={"owner": lax.rem(me + d, n)})
    pl.semaphore_wait(barrier, n - 1)

    def slot_copy(k, j):
        return pltpu.make_async_remote_copy(
            src_ref=pack_ref.at[base + j], dst_ref=recv_ref.at[chips - k - 1, j, pl.ds(upper, half)],
            send_sem=slot_send.at[k, j], recv_sem=slot_recv.at[k, j],
            device_id={"owner": lax.rem(me + 2 * k, n)},
        )

    def forward(k, j):
        return pltpu.make_async_remote_copy(
            src_ref=recv_ref.at[chips - k - 1, j, pl.ds(upper, half)],
            dst_ref=recv_ref.at[chips - k - 1, j, pl.ds(upper, half)],
            send_sem=fwd_send.at[k, j], recv_sem=fwd_recv.at[k, j], device_id={"owner": sibling},
        )

    for j in range(count):
        for k in range(1, chips):
            slot_copy(k, j).start()
    for j in range(count):
        for k in range(1, chips):
            slot_copy(k, j).wait_recv()
            forward(k, j).start()
    for j in range(count):
        for k in range(1, chips):
            slot_copy(k, j).wait_send()
            forward(k, j).wait()


def finish_kernel(blocks, base, work_ref, unit, acc, dens, *refs):
    recvs = refs[: 2 if base else 1]
    out_ref, log_ref, near, reach, density, out, out_sem = refs[len(recvs):]
    first = recvs[0].shape[1]

    def store(i):
        return pltpu.make_async_copy(out.at[i], out_ref.at[i], out_sem.at[i])

    def meet(i, other):
        weights = kernel_of(unit[i], other)
        reach[...] += jnp.broadcast_to(jnp.sum(weights, axis=1, keepdims=True), (BLOCK, LANES))
        near[...] += jnp.dot(weights.astype(BF16), other, preferred_element_type=F32)

    def close(i, total, sums):
        share = total * (1.0 / sums[:, 0:1])
        out[i] = (unit[i].astype(F32) - share).astype(BF16)
        store(i).start()
        density[...] = jnp.where(iota((BLOCK, LANES), 1) == i, sums, density[...])

    density[...] = jnp.ones_like(density)

    @pl.loop(0, blocks)
    def _(i):
        number = work_ref[i, LANES - 1]

        @pl.when(number == 0)
        def _():
            close(i, acc[i], dens[i])

        @pl.when(number > 0)
        def _():
            near[...] = acc[i]
            reach[...] = dens[i]

            @pl.loop(0, number)
            def _(t):
                code = work_ref[i, t]
                chip, spot = code // (2 * blocks), lax.rem(code, 2 * blocks)
                if base:
                    @pl.when(spot < first)
                    def _():
                        meet(i, recvs[0][chip, jnp.minimum(spot, first - 1)])

                    @pl.when(spot >= first)
                    def _():
                        meet(i, recvs[1][chip, jnp.maximum(spot - first, 0)])
                else:
                    meet(i, recvs[0][chip, jnp.minimum(spot, first - 1)])

            close(i, near[...], reach[...])

    log_ref[...] = jnp.log(density[...].T[0:blocks])

    for i in range(blocks):
        store(i).wait()


def shards(groups, embeddings, home_pairs, home_count, surplus_pairs):
    n = lax.axis_size("owner")
    chips = n // 2
    width = embeddings.shape[1]
    blocks = embeddings.shape[0] // BLOCK
    shifts = home_pairs.shape[2]
    most = 2 * blocks
    extra = tuple(e for e in EXTRA if FIRST + e < most) + (most - FIRST,)
    limits = (FIRST,) + tuple(FIRST + e for e in extra[:-1])

    pairs = home_pairs[0, 0].transpose(0, 2, 1)
    count = home_count[0, 0].reshape(1, shifts)
    chosen = surplus_pairs.transpose(0, 3, 1, 2)
    emb = embeddings.reshape(blocks, BLOCK, width)
    vmem = pl.BlockSpec(memory_space=VMEM)
    smem = pl.BlockSpec(memory_space=SMEM)
    anyw = pl.BlockSpec(memory_space=ANY)
    shape = jax.ShapeDtypeStruct
    dma = pltpu.SemaphoreType.DMA
    half = BLOCK // 2
    steps = groups.bit_length() - 1

    unit, acc, dens, pack, recv, work, level = pl.pallas_call(
        functools.partial(front_kernel, n, groups, shifts, limits),
        out_shape=(
            shape((blocks, BLOCK, width), BF16),
            shape((blocks, BLOCK, width), F32),
            shape((blocks, BLOCK, LANES), F32),
            shape((2 * blocks, half, width), BF16),
            shape((chips - 1, FIRST, BLOCK, width), BF16),
            shape((blocks, LANES), I32),
            shape((1,), I32),
        ),
        in_specs=[vmem, vmem, vmem, pl.BlockSpec(memory_space=pltpu.MemorySpace.HBM)],
        out_specs=(vmem, vmem, vmem, anyw, vmem, vmem, smem),
        scratch_shapes=[
            pltpu.VMEM((blocks, BLOCK, width), BF16),
            pltpu.VMEM((2 * blocks, half, width), BF16),
            pltpu.VMEM((blocks, half, width), BF16),
            pltpu.VMEM((2 * blocks, half, width), BF16),
            pltpu.VMEM((LANES // blocks, blocks, LANES), F32),
            pltpu.VMEM((blocks, 1, blocks * BLOCK), F32),
            pltpu.VMEM((blocks, 1, blocks * half), F32),
            pltpu.VMEM((steps + 1, blocks, LANES), F32),
            pltpu.VMEM((steps, blocks, LANES), F32),
            dma((blocks,)), dma((blocks,)), dma((blocks,)), dma((blocks,)), dma((blocks,)),
            dma((n,)), dma((n,)),
            dma((chips, FIRST)), dma((chips, FIRST)), dma((chips, FIRST)), dma((chips, FIRST)),
            dma((steps,)), dma((steps,)), dma,
        ],
        compiler_params=pltpu.CompilerParams(
            collective_id=0, has_side_effects=True, vmem_limit_bytes=FRONT_BYTES
        ),
    )(pairs, count, chosen, emb)

    def finish(base, recvs, work, unit, acc, dens):
        centered, log_density = pl.pallas_call(
            functools.partial(finish_kernel, blocks, base),
            out_shape=(
                shape((blocks, BLOCK, width), BF16),
                shape((blocks, BLOCK), F32),
            ),
            in_specs=[smem] + [vmem] * (3 + len(recvs)),
            out_specs=(anyw, vmem),
            scratch_shapes=[
                pltpu.VMEM((BLOCK, width), F32),
                pltpu.VMEM((BLOCK, LANES), F32),
                pltpu.VMEM((BLOCK, LANES), F32),
                pltpu.VMEM((blocks, BLOCK, width), BF16),
                dma((blocks,)),
            ],
            compiler_params=pltpu.CompilerParams(vmem_limit_bytes=VMEM_BYTES),
        )(work, unit, acc, dens, *recvs)
        return centered.reshape(-1, width), log_density.reshape(-1)

    def enough(work, unit, acc, dens, pack, recv):
        return finish(0, (recv,), work, unit, acc, dens)

    def with_more(rank, number, work, unit, acc, dens, pack, recv):
        later = pl.pallas_call(
            functools.partial(more_kernel, n, FIRST, number),
            out_shape=shape((chips - 1, number, BLOCK, width), BF16),
            in_specs=[anyw],
            out_specs=anyw,
            scratch_shapes=[dma((chips, number)) for _ in range(4)],
            compiler_params=pltpu.CompilerParams(
                collective_id=1 + rank, has_side_effects=True, vmem_limit_bytes=4 * 1024 * 1024
            ),
        )(pack)
        return finish(FIRST, (recv, later), work, unit, acc, dens)

    branches = [enough] + [functools.partial(with_more, rank, e) for rank, e in enumerate(extra)]
    return lax.switch(level[0], branches, work, unit, acc, dens, pack, recv)


def solution(mesh):
    return jax.shard_map(
        functools.partial(shards, mesh.shape["group"]),
        mesh=mesh,
        in_specs=(
            P(("group", "owner"), None),
            P("group", "owner", None, None, None),
            P("group", "owner", None),
            P("group", "owner", None, None),
        ),
        out_specs=(P(("group", "owner"), None), P(("group", "owner"))),
        check_vma=False,
    )
```
